1024 devices in a mesh: dp: 64 (over z, y), tensor: 16 (over x, core).
Axes of the slice: x: 8, y: 8, z: 8, core: 2. Of those that a mesh axis runs over, the one named last changes fastest.
Arguments:
- hidden: bfloat16 [8192, 12288], P('dp', 'tensor'), may hold values from -6 to 6
- cotangent: bfloat16 [8192, 4096], P('dp', 'tensor'), may hold values from -6 to 6
- blocks: bfloat16 [1024, 128, 128], P('tensor'), may hold values from -0.09375 to 0.09375
- block_pos: int32 [16, 64], P('tensor'), may hold values from 0 to 191, as said below
- owner_rank: int32 [16, 64], P('tensor'), may hold values from 0 to 63, each once within a row
- moment: float32 [16, 64, 128, 128], P('tensor', 'dp'), may hold values from -0.009943689 to 0.009943689
- second: float32 [16, 64, 128, 128], P('tensor', 'dp'), may hold values from 3.0517577e-07 to 4.8828124e-06
Outputs:
- mixed: bfloat16 [8192, 4096], P('dp', 'tensor')
- hidden_grad: bfloat16 [8192, 12288], P('dp', 'tensor')
- new_moment: float32 [16, 64, 128, 128], P('tensor', 'dp')
- new_second: float32 [16, 64, 128, 128], P('tensor', 'dp')
- direction: float32 [16, 64, 128, 128], P('tensor', 'dp')
- new_blocks: bfloat16 [1024, 128, 128], P('tensor')
The draws below stay inside these ranges and needn't reach their ends.
Inputs may be any that keep to these rules, and one draw needn't show every extreme that they name: `block_pos`: each row holds 64 different positions of the 6 x 32 blocks of one slab, in no order. `owner_rank`: the block of rank k has its optimizer state at dp index k.
All inputs are finite; a program needn't handle non-finite values.
Results may differ from the reference program's by a relative error of at most 0.017.
Values may be sent and summed in bfloat16 or wider, within the bound.
No kernel may reach another device: no remote copies, remote signals or barrier semaphores. Data moves between devices by JAX's collectives and lax.ppermute only.
A program may use at most 64 MiB of HBM per device.

```python
import math
import jax
import jax.numpy as jnp
from jax import lax

D = 4096
FF_DEV = 768
BS = 128
SLOTS = 64
FF = 12288
TOKENS = 8192
N_TENSOR = 16


def draw_block_pos(key, part):
    row_keys = jax.random.split(jax.random.fold_in(key, 7), N_TENSOR)

    def one_row(row_key):
        return jax.random.permutation(row_key, FF_DEV // BS * (D // BS))[:SLOTS]
    return jax.vmap(one_row)(row_keys).astype(jnp.int32)


def steps_of(rng, dims, cuts, low, largest):
    gain, own = 1.0, jax.random.fold_in(rng, 6)
    for dim, parts in cuts:
        draws = jnp.exp(jax.random.uniform(jax.random.fold_in(own, dim), (parts,), jnp.float32, low / len(cuts), largest / len(cuts)))
        gain = gain * jnp.repeat(draws, dims[dim] // parts).reshape([-1 if axis == dim else 1 for axis in range(len(dims))])
    return gain


def bell_draw(key, extent, spread, reach, shards=(), kind=jnp.bfloat16):
    array = spread * jax.random.normal(key, extent, jnp.float32)
    if shards:
        array = array * steps_of(key, extent, shards, -0.22, 0.18)
    return jnp.clip(array, -reach, reach).astype(kind)


def setup_inputs(seed: int = 0) -> dict:
    arg_keys = jax.random.split(jax.random.key(seed), 8)
    hidden = bell_draw(arg_keys[0], (TOKENS, FF), 1.0, 6.0, ((0, 64), (1, 16)))
    cotangent = bell_draw(arg_keys[1], (TOKENS, D), 1.0, 6.0, ((0, 64), (1, 16)))
    blocks = bell_draw(arg_keys[2], (N_TENSOR * SLOTS, BS, BS), (BS * SLOTS * N_TENSOR // (D // BS)) ** -0.5, 0.09375, ((0, 16),))
    block_pos = draw_block_pos(jax.random.fold_in(arg_keys[7], 71), 0)
    owner_rank = jax.vmap(lambda own: jax.random.permutation(own, SLOTS))(jax.random.split(arg_keys[4], N_TENSOR)).reshape((N_TENSOR, SLOTS)).astype(jnp.int32)
    moment = bell_draw(arg_keys[5], (N_TENSOR, SLOTS, BS, BS), (0.15 * TOKENS ** -0.5), 0.009943689, ((0, 16), (1, 64)), jnp.float32)
    second = jnp.clip(jnp.exp(math.log(4.882812390860636e-06) - 2.7725887 * jax.random.uniform(arg_keys[6], (N_TENSOR, SLOTS, BS, BS), jnp.float32) ** steps_of(arg_keys[6], (N_TENSOR, SLOTS, BS, BS), ((0, 16), (1, 64)), -0.2, 0.2)), 3.0517577442878974e-07, 4.882812390860636e-06)
    return dict(hidden=hidden, cotangent=cotangent, blocks=blocks, block_pos=block_pos, owner_rank=owner_rank, moment=moment, second=second)


def reference(hidden, cotangent, blocks, block_pos, owner_rank, moment, second):
    fblk = FF_DEV // BS
    dblk = D // BS
    hid_slabs = hidden.reshape(TOKENS, N_TENSOR, fblk, BS).transpose(1, 0, 2, 3)
    grad_blocks = cotangent.reshape(TOKENS, dblk, BS).astype(jnp.float32)
    slab_blocks = blocks.reshape(N_TENSOR, SLOTS, BS, BS)
    highest = lax.Precision.HIGHEST

    def one_slab(carry, inputs):
        hid_t, blk_t, pos_t, rank_t, mom_t, sec_t = inputs
        block_rows = (pos_t // dblk).astype(jnp.int32)
        block_cols = (pos_t % dblk).astype(jnp.int32)
        chosen_hid = jnp.take(hid_t, block_rows, axis=1).astype(jnp.float32)
        chosen_grad = jnp.take(grad_blocks, block_cols, axis=1)
        weights = blk_t.astype(jnp.float32)
        col_hot = (block_cols[:, None] == jnp.arange(dblk)[None, :]).astype(jnp.float32)
        row_hot = (block_rows[:, None] == jnp.arange(fblk)[None, :]).astype(jnp.float32)
        contrib = jnp.einsum('nsa,sab->nsb', chosen_hid, weights, precision=highest)
        partial_value = jnp.einsum('nsb,sc->ncb', contrib, col_hot, precision=highest).reshape(TOKENS, D)
        partial_value = lax.optimization_barrier(partial_value.astype(jnp.bfloat16)).astype(jnp.float32)
        back = jnp.einsum('nsb,sab->nsa', chosen_grad, weights, precision=highest)
        hid_grad = jnp.einsum('nsa,sr->nra', back, row_hot, precision=highest).reshape(TOKENS, FF_DEV).astype(jnp.bfloat16)
        grads = jnp.einsum('nsa,nsb->sab', chosen_hid, chosen_grad, precision=highest) * (1.0 / TOKENS)
        order = jnp.argsort(rank_t).astype(jnp.int32)
        grads_ranked = jnp.take(grads, order, axis=0)
        weights_ranked = jnp.take(weights, order, axis=0)
        mom_next = 0.9 * mom_t + 0.1 * grads_ranked
        sec_next = 0.999 * sec_t + 0.001 * grads_ranked * grads_ranked
        step_dir = mom_next / (jnp.sqrt(sec_next) + 1e-08)
        updated = (weights_ranked - 0.002 * (step_dir + 0.1 * weights_ranked)).astype(jnp.bfloat16)
        listed = jnp.take(updated, rank_t.astype(jnp.int32), axis=0)
        return (carry + partial_value, (hid_grad, mom_next, sec_next, step_dir, listed))
    start = jnp.zeros((TOKENS, D), jnp.float32)
    total, outs = lax.scan(one_slab, start, (hid_slabs, slab_blocks, block_pos, owner_rank, moment, second))
    hid_grads, new_moment, new_second, direction, listed = outs
    mixed = total.astype(jnp.bfloat16)
    hidden_grad = hid_grads.transpose(1, 0, 2).reshape(TOKENS, N_TENSOR * FF_DEV)
    new_blocks = listed.reshape(N_TENSOR * SLOTS, BS, BS)
    return (mixed, hidden_grad, new_moment, new_second, direction, new_blocks)
```

```python
import functools

import jax
import jax.numpy as jnp
from jax import lax
from jax.experimental import pallas as pl
from jax.experimental.pallas import tpu as pltpu
from jax.sharding import Mesh
from jax.sharding import PartitionSpec as P

DP = ("dp_0", "dp_1")
TENSOR = ("x", "core")
VMEM = pl.BlockSpec(memory_space=pltpu.VMEM)
SMEM = pl.BlockSpec(memory_space=pltpu.SMEM)
BF = jnp.bfloat16
F32 = jnp.float32


def call(kernel, out_shape, n_smem, n_vmem, scratch=(), flops=0, nbytes=0):
    n_out = len(jax.tree.leaves(out_shape))
    return pl.pallas_call(
        kernel,
        out_shape=out_shape,
        in_specs=[SMEM] * n_smem + [VMEM] * n_vmem,
        out_specs=VMEM if n_out == 1 else [VMEM] * n_out,
        scratch_shapes=list(scratch),
        cost_estimate=pl.CostEstimate(flops=flops, bytes_accessed=nbytes, transcendentals=0),
    )


def aligned(index, size):
    return pl.ds(pl.multiple_of(index * size, size), size)


def fill_slab(pos_ref, blocks_ref, slab):
    slots, bs, _ = blocks_ref.shape
    rows, width = slab.shape
    col_blocks = width // bs

    def clear(i, carry):
        slab[aligned(i, 16), :] = jnp.zeros((16, width), BF)
        return carry

    lax.fori_loop(0, rows // 16, clear, 0, unroll=2)

    def place(s, carry):
        p = pos_ref[0, s]
        slab[aligned(p // col_blocks, bs), aligned(p % col_blocks, bs)] = blocks_ref[s]
        return carry

    lax.fori_loop(0, slots, place, 0, unroll=4)


def partial_kernel(core_ref, pos_ref, hid_ref, blocks_ref, out_ref, slab):
    feats = out_ref.shape[-1]
    fill_slab(pos_ref, blocks_ref, slab)
    hid = hid_ref[...]

    def step(t, carry):
        value = jnp.dot(hid, slab[:, aligned(t, feats)], preferred_element_type=F32)
        out_ref[(t % 2) ^ core_ref[0], t // 2] = value.astype(BF)
        return carry

    lax.fori_loop(0, slab.shape[1] // feats, step, 0, unroll=2)


def join_features(core_ref, own_ref, other_ref, full):
    pieces, _, feats = own_ref.shape
    core = core_ref[0]
    for j in range(pieces):
        full[:, aligned(2 * j + core, feats)] = own_ref[j]
        full[:, aligned(2 * j + 1 - core, feats)] = other_ref[j]


def place_of(rank, core, side):
    return jnp.where(core == 0, rank, (rank % side) * side + rank // side)


def grads_kernel(side, factor, core_ref, pos_ref, rank_ref, hid_ref, own_ref, other_ref, out_ref, full, hid_t):
    slots, bs, _ = out_ref.shape
    col_blocks = full.shape[1] // bs
    core = core_ref[0]
    join_features(core_ref, own_ref, other_ref, full)
    hid_t[...] = hid_ref[...].T

    def step(s, carry):
        p = pos_ref[0, s]
        value = jnp.dot(
            hid_t[aligned(p // col_blocks, bs), :],
            full[:, aligned(p % col_blocks, bs)],
            preferred_element_type=F32,
        )
        out_ref[place_of(rank_ref[0, s], core, side)] = (value * factor).astype(BF)
        return carry

    lax.fori_loop(0, slots, step, 0, unroll=8)


def back_kernel(core_ref, owner_ref, pos_ref, rank_ref, own_ref, other_ref, blocks_ref, out_ref, mine_ref, full, slab):
    slots, bs, _ = blocks_ref.shape
    join_features(core_ref, own_ref, other_ref, full)
    fill_slab(pos_ref, blocks_ref, slab)

    def find(s, found):
        return jnp.where(rank_ref[0, s] == owner_ref[0], s, found)

    mine_ref[...] = blocks_ref[lax.fori_loop(0, slots, find, 0)]
    value = full[...]
    step = 2 * bs
    for n in range(slab.shape[0] // step):
        rows = slab[n * step : (n + 1) * step, :]
        out_ref[:, n * step : (n + 1) * step] = lax.dot_general(
            value, rows, (((1,), (1,)), ((), ())), preferred_element_type=F32
        ).astype(BF)


def list_kernel(side, core_ref, rank_ref, in_ref, out_ref):
    core = core_ref[0]

    def step(s, carry):
        out_ref[s] = in_ref[place_of(rank_ref[0, s], core, side)]
        return carry

    lax.fori_loop(0, out_ref.shape[0], step, 0, unroll=4)


def chip_groups(sizes):
    n0, n1, nx, nc = sizes

    def at(z, y, x, c):
        return ((z * n1 + y) * nx + x) * nc + c

    along_0 = lambda c: [[at(z, y, x, c) for z in range(n0)] for y in range(n1) for x in range(nx)]
    along_1 = lambda c: [[at(z, y, x, c) for y in range(n1)] for z in range(n0) for x in range(nx)]
    return along_0(0) + along_1(1), along_1(0) + along_0(1)


def shards(sizes, hidden, cotangent, blocks, block_pos, owner_rank, moment, second):
    tokens, feats = cotangent.shape
    rows = hidden.shape[1]
    slots, bs, _ = blocks.shape
    n0, n1, nx, nc = sizes
    width = feats * nx * nc
    axes = (*DP, *TENSOR)
    first, then = chip_groups(sizes)
    core = lax.axis_index("core").reshape(1)
    owner = lax.axis_index(DP).reshape(1)
    swap = [(0, 1), (1, 0)]
    factor = 1.0 / (tokens * n0 * n1)

    def exchange(value, groups):
        return lax.all_to_all(value, axes, 0, 0, axis_index_groups=groups, tiled=True)

    partials = call(
        partial_kernel,
        jax.ShapeDtypeStruct((nc, nx, tokens, feats), BF),
        2,
        2,
        [pltpu.VMEM((rows, width), BF)],
        flops=2 * tokens * rows * width,
        nbytes=4 * 2**20,
    )(core, block_pos, hidden, blocks)
    theirs = lax.ppermute(partials[1], "core", swap)
    pair = (partials[0].astype(F32) + theirs.astype(F32)).astype(BF)
    sent = jnp.concatenate([jnp.broadcast_to(cotangent, pair.shape), pair], axis=1)
    came = lax.all_to_all(sent, "x", 0, 0, tiled=True)
    mixed = came[:, tokens:].astype(F32).sum(axis=0).astype(BF)
    own = came[:, :tokens]
    other = lax.ppermute(own, "core", swap)

    grads = call(
        functools.partial(grads_kernel, n0, factor),
        jax.ShapeDtypeStruct((slots, bs, bs), BF),
        3,
        3,
        [pltpu.VMEM((tokens, width), BF), pltpu.VMEM((rows, tokens), BF)],
        flops=2 * tokens * bs * bs * slots,
        nbytes=4 * 2**20,
    )(core, block_pos, owner_rank, hidden, own, other)
    hidden_grad, mine = call(
        back_kernel,
        (jax.ShapeDtypeStruct((tokens, rows), BF), jax.ShapeDtypeStruct((bs, bs), BF)),
        4,
        3,
        [pltpu.VMEM((tokens, width), BF), pltpu.VMEM((rows, width), BF)],
        flops=2 * tokens * rows * width,
        nbytes=4 * 2**20,
    )(core, owner, block_pos, owner_rank, own, other, blocks)

    got = exchange(grads.reshape(n0, slots // n0, bs, bs), first)
    part = got.astype(F32).sum(axis=0).astype(BF)
    grad = exchange(part, then).astype(F32).sum(axis=0)
    weight = mine.astype(F32)
    mom_next = 0.9 * moment[0, 0] + 0.1 * grad
    sec_next = 0.999 * second[0, 0] + 0.001 * grad * grad
    step_dir = mom_next / (jnp.sqrt(sec_next) + 1e-08)
    updated = (weight - 0.002 * (step_dir + 0.1 * weight)).astype(BF)
    row = exchange(jnp.broadcast_to(updated, (n1, bs, bs)), then)
    every = exchange(jnp.broadcast_to(row, (n0, n1, bs, bs)), first)
    new_blocks = call(
        functools.partial(list_kernel, n0),
        jax.ShapeDtypeStruct((slots, bs, bs), BF),
        2,
        1,
        nbytes=4 * 2**20,
    )(core, owner_rank, every.reshape(slots, bs, bs))
    return (mixed, hidden_grad, mom_next[None, None], sec_next[None, None], step_dir[None, None], new_blocks)


def make(sizes, torus):
    placed = (
        P(DP, TENSOR),
        P(DP, TENSOR),
        P(TENSOR, None, None),
        P(TENSOR, None),
        P(TENSOR, None),
        P(TENSOR, DP, None, None),
        P(TENSOR, DP, None, None),
    )
    return jax.shard_map(
        functools.partial(shards, sizes),
        mesh=torus,
        in_specs=placed,
        out_specs=(
            P(DP, TENSOR),
            P(DP, TENSOR),
            P(TENSOR, DP, None, None),
            P(TENSOR, DP, None, None),
            P(TENSOR, DP, None, None),
            P(TENSOR, None, None),
        ),
        check_vma=False,
    )


def solution(mesh):
    sizes = (8, mesh.shape["dp"] // 8, mesh.shape["tensor"] // 2, 2)
    return make(sizes, Mesh(mesh.devices.reshape(sizes), (*DP, *TENSOR)))
```

```python
import functools

import jax
import jax.numpy as jnp
from jax import lax
from jax.experimental import pallas as pl
from jax.experimental.pallas import tpu as pltpu
from jax.sharding import Mesh
from jax.sharding import PartitionSpec as P

DP = ("dp_0", "dp_1")
TENSOR = ("x", "core")
VMEM = pl.BlockSpec(memory_space=pltpu.VMEM)
SMEM = pl.BlockSpec(memory_space=pltpu.SMEM)
ANY = pl.BlockSpec(memory_space=pl.ANY)
BF = jnp.bfloat16
F32 = jnp.float32


def call(kernel, out_shape, ins, outs, scratch=(), flops=0, nbytes=0, limit=24):
    return pl.pallas_call(
        kernel,
        out_shape=out_shape,
        in_specs=ins,
        out_specs=outs,
        scratch_shapes=list(scratch),
        cost_estimate=pl.CostEstimate(flops=flops, bytes_accessed=nbytes, transcendentals=0),
        compiler_params=pltpu.CompilerParams(vmem_limit_bytes=limit * 2**20),
    )


def aligned(index, size):
    return pl.ds(pl.multiple_of(index * size, size), size)


def fill_slab(pos_ref, blocks_ref, slab):
    slots, bs, _ = blocks_ref.shape
    rows, width = slab.shape
    col_blocks = width // bs

    def clear(i, carry):
        slab[aligned(i, 16), :] = jnp.zeros((16, width), BF)
        return carry

    lax.fori_loop(0, rows // 16, clear, 0, unroll=2)

    def place(s, carry):
        p = pos_ref[0, s]
        slab[aligned(p // col_blocks, bs), aligned(p % col_blocks, bs)] = blocks_ref[s]
        return carry

    lax.fori_loop(0, slots, place, 0, unroll=4)


def partial_kernel(place_ref, pos_ref, hid_ref, blocks_ref, keep_ref, send_ref, slab):
    chips, _, feats = keep_ref.shape
    bits = chips.bit_length() - 1
    x, core = place_ref[0], place_ref[1]
    fill_slab(pos_ref, blocks_ref, slab)
    hid = hid_ref[...]
    for i in range(chips):
        r = sum(((i >> b) & 1) << (bits - 1 - b) for b in range(bits))
        chip = x ^ r
        for ref, c in ((keep_ref, core), (send_ref, 1 - core)):
            value = jnp.dot(hid, slab[:, aligned(2 * chip + c, feats)], preferred_element_type=F32)
            ref[i] = value.astype(BF)


def join_features(core, own_ref, other_ref, full, sems):
    pieces, _, feats = own_ref.shape
    copies = []
    for j in range(pieces):
        for k, (ref, c) in enumerate(((own_ref, core), (other_ref, 1 - core))):
            copies.append(pltpu.make_async_copy(ref.at[j], full.at[:, aligned(2 * j + c, feats)], sems.at[k, j]))
    for copy in copies:
        copy.start()
    return copies


def place_of(rank, core, side):
    return jnp.where(core == 0, rank, (rank % side) * side + rank // side)


def grads_kernel(side, factor, place_ref, pos_ref, rank_ref, hid_ref, own_ref, other_ref, out_ref, full, hid_t, sems):
    slots, bs, _ = out_ref.shape
    col_blocks = full.shape[1] // bs
    core = place_ref[1]
    copies = join_features(core, own_ref, other_ref, full, sems)
    hid_t[...] = hid_ref[...].T
    for copy in copies:
        copy.wait()

    def step(s, carry):
        p = pos_ref[0, s]
        value = jnp.dot(
            hid_t[aligned(p // col_blocks, bs), :],
            full[:, aligned(p % col_blocks, bs)],
            preferred_element_type=F32,
        )
        out_ref[place_of(rank_ref[0, s], core, side)] = (value * factor).astype(BF)
        return carry

    lax.fori_loop(0, slots, step, 0, unroll=8)


def back_kernel(place_ref, pos_ref, rank_ref, blocks_ref, own_ref, other_ref, out_ref, mine_ref, full, slab, sems):
    slots, bs, _ = blocks_ref.shape
    copies = join_features(place_ref[1], own_ref, other_ref, full, sems)
    fill_slab(pos_ref, blocks_ref, slab)

    def find(s, found):
        return jnp.where(rank_ref[0, s] == place_ref[2], s, found)

    mine_ref[...] = blocks_ref[lax.fori_loop(0, slots, find, 0)]
    for copy in copies:
        copy.wait()
    value = full[...]
    step = 2 * bs
    for n in range(slab.shape[0] // step):
        rows = slab[n * step : (n + 1) * step, :]
        out_ref[:, n * step : (n + 1) * step] = lax.dot_general(
            value, rows, (((1,), (1,)), ((), ())), preferred_element_type=F32
        ).astype(BF)


def list_kernel(side, place_ref, rank_ref, in_ref, out_ref, sems):
    core = place_ref[1]
    slots = out_ref.shape[0]

    def copy(s):
        return pltpu.make_async_copy(in_ref.at[place_of(rank_ref[0, s], core, side)], out_ref.at[s], sems.at[s])

    def start(s, carry):
        copy(s).start()
        return carry

    def wait(s, carry):
        copy(s).wait()
        return carry

    lax.fori_loop(0, slots, start, 0, unroll=4)
    lax.fori_loop(0, slots, wait, 0, unroll=4)


def chip_groups(sizes):
    n0, n1, nx, nc = sizes

    def at(z, y, x, c):
        return ((z * n1 + y) * nx + x) * nc + c

    along_0 = lambda c: [[at(z, y, x, c) for z in range(n0)] for y in range(n1) for x in range(nx)]
    along_1 = lambda c: [[at(z, y, x, c) for y in range(n1)] for z in range(n0) for x in range(nx)]
    return along_0(0) + along_1(1), along_1(0) + along_0(1)


def shards(sizes, hidden, cotangent, blocks, block_pos, owner_rank, moment, second):
    tokens, feats = cotangent.shape
    rows = hidden.shape[1]
    slots, bs, _ = blocks.shape
    n0, n1, nx, nc = sizes
    width = feats * nx * nc
    axes = (*DP, *TENSOR)
    first, then = chip_groups(sizes)
    place = jnp.stack([lax.axis_index("x"), lax.axis_index("core"), lax.axis_index(DP)])
    swap = [(0, 1), (1, 0)]
    factor = 1.0 / (tokens * n0 * n1)
    block_list = jax.ShapeDtypeStruct((slots, bs, bs), BF)

    def exchange(value, groups):
        return lax.all_to_all(value, axes, 0, 0, axis_index_groups=groups, tiled=True)

    own = lax.all_to_all(jnp.broadcast_to(cotangent, (nx, tokens, feats)), "x", 0, 0, tiled=True)
    keep, send = call(
        partial_kernel,
        (jax.ShapeDtypeStruct((nx, tokens, feats), BF),) * 2,
        [SMEM, SMEM, VMEM, VMEM],
        [VMEM, VMEM],
        [pltpu.VMEM((rows, width), BF)],
        flops=2 * tokens * rows * width,
        nbytes=4 * 2**20,
    )(place, block_pos, hidden, blocks)
    total = keep.astype(F32) + lax.ppermute(send, "core", swap).astype(F32)
    total = total.astype(BF)
    own, total = lax.optimization_barrier((own, total))
    other = lax.ppermute(own, "core", swap)

    def halved(value, step):
        half = value.shape[0] // 2
        theirs = lax.ppermute(value[half:], "x", [(i, i ^ step) for i in range(nx)])
        return (value[:half].astype(F32) + theirs.astype(F32)).astype(BF)

    total = halved(total, 1)

    grads = call(
        functools.partial(grads_kernel, n0, factor),
        block_list,
        [SMEM, SMEM, SMEM, VMEM, ANY, ANY],
        VMEM,
        [pltpu.VMEM((tokens, width), BF), pltpu.VMEM((rows, tokens), BF), pltpu.SemaphoreType.DMA((2, nx))],
        flops=2 * tokens * bs * bs * slots,
        nbytes=4 * 2**20,
    )(place, block_pos, owner_rank, hidden, own, other)
    hidden_grad, mine = call(
        back_kernel,
        (jax.ShapeDtypeStruct((tokens, rows), BF), jax.ShapeDtypeStruct((bs, bs), BF)),
        [SMEM, SMEM, SMEM, VMEM, ANY, ANY],
        [VMEM, VMEM],
        [pltpu.VMEM((tokens, width), BF), pltpu.VMEM((rows, width), BF), pltpu.SemaphoreType.DMA((2, nx))],
        flops=2 * tokens * rows * width,
        nbytes=4 * 2**20,
    )(place, block_pos, owner_rank, blocks, own, other)

    got = exchange(grads.reshape(n0, slots // n0, bs, bs), first)
    got, mine, total = lax.optimization_barrier((got, mine, total))
    step = 2
    while total.shape[0] > 1:
        total = halved(total, step)
        step *= 2
    mixed = total[0]
    part = got.astype(F32).sum(axis=0).astype(BF)
    grad = exchange(part, then).astype(F32).sum(axis=0)
    weight = mine.astype(F32)
    mom_next = 0.9 * moment[0, 0] + 0.1 * grad
    sec_next = 0.999 * second[0, 0] + 0.001 * grad * grad
    step_dir = mom_next / (jnp.sqrt(sec_next) + 1e-08)
    updated = (weight - 0.002 * (step_dir + 0.1 * weight)).astype(BF)
    row = exchange(jnp.broadcast_to(updated, (n1, bs, bs)), then)
    every = exchange(jnp.broadcast_to(row, (n0, n1, bs, bs)), first)
    new_blocks = call(
        functools.partial(list_kernel, n0),
        block_list,
        [SMEM, SMEM, ANY],
        ANY,
        [pltpu.SemaphoreType.DMA((slots,))],
        nbytes=4 * 2**20,
        limit=4,
    )(place, owner_rank, every.reshape(slots, bs, bs))
    return (mixed, hidden_grad, mom_next[None, None], sec_next[None, None], step_dir[None, None], new_blocks)


def make(sizes, torus):
    placed = (
        P(DP, TENSOR),
        P(DP, TENSOR),
        P(TENSOR, None, None),
        P(TENSOR, None),
        P(TENSOR, None),
        P(TENSOR, DP, None, None),
        P(TENSOR, DP, None, None),
    )
    return jax.shard_map(
        functools.partial(shards, sizes),
        mesh=torus,
        in_specs=placed,
        out_specs=(
            P(DP, TENSOR),
            P(DP, TENSOR),
            P(TENSOR, DP, None, None),
            P(TENSOR, DP, None, None),
            P(TENSOR, DP, None, None),
            P(TENSOR, None, None),
        ),
        check_vma=False,
    )


def solution(mesh):
    sizes = (8, mesh.shape["dp"] // 8, mesh.shape["tensor"] // 2, 2)
    return make(sizes, Mesh(mesh.devices.reshape(sizes), (*DP, *TENSOR)))
```

```python
import functools

import jax
import jax.numpy as jnp
from jax import lax
from jax.experimental import pallas as pl
from jax.experimental.pallas import tpu as pltpu
from jax.sharding import Mesh
from jax.sharding import PartitionSpec as P

DP = ("dp_0", "dp_1")
TENSOR = ("x", "core")
VMEM = pl.BlockSpec(memory_space=pltpu.VMEM)
SMEM = pl.BlockSpec(memory_space=pltpu.SMEM)
ANY = pl.BlockSpec(memory_space=pl.ANY)
BF = jnp.bfloat16
F32 = jnp.float32


def call(kernel, out_shape, ins, outs, scratch=(), flops=0, nbytes=0, limit=24):
    return pl.pallas_call(
        kernel,
        out_shape=out_shape,
        in_specs=ins,
        out_specs=outs,
        scratch_shapes=list(scratch),
        cost_estimate=pl.CostEstimate(flops=flops, bytes_accessed=nbytes, transcendentals=0),
        compiler_params=pltpu.CompilerParams(vmem_limit_bytes=limit * 2**20),
    )


def aligned(index, size):
    return pl.ds(pl.multiple_of(index * size, size), size)


def fill_slab(pos_ref, blocks_ref, slab):
    slots, bs, _ = blocks_ref.shape
    rows, width = slab.shape
    col_blocks = width // bs

    def clear(i, carry):
        slab[aligned(i, 16), :] = jnp.zeros((16, width), BF)
        return carry

    lax.fori_loop(0, rows // 16, clear, 0, unroll=2)

    def place(s, carry):
        p = pos_ref[0, s]
        slab[aligned(p // col_blocks, bs), aligned(p % col_blocks, bs)] = blocks_ref[s]
        return carry

    lax.fori_loop(0, slots, place, 0, unroll=4)


def partial_kernel(place_ref, pos_ref, rank_ref, hid_ref, blocks_ref, keep_ref, send_ref, mine_ref, slab):
    chips, _, feats = keep_ref.shape
    bits = chips.bit_length() - 1
    x, core = place_ref[0], place_ref[1]
    fill_slab(pos_ref, blocks_ref, slab)

    def find(s, found):
        return jnp.where(rank_ref[0, s] == place_ref[2], s, found)

    mine_ref[...] = blocks_ref[lax.fori_loop(0, blocks_ref.shape[0], find, 0)]
    hid = hid_ref[...]
    for i in range(chips):
        r = sum(((i >> b) & 1) << (bits - 1 - b) for b in range(bits))
        chip = x ^ r
        for ref, c in ((keep_ref, core), (send_ref, 1 - core)):
            value = jnp.dot(hid, slab[:, aligned(2 * chip + c, feats)], preferred_element_type=F32)
            ref[i] = value.astype(BF)


def join_features(core, own_ref, other_ref, full, sems):
    pieces, _, feats = own_ref.shape
    copies = []
    for j in range(pieces):
        for k, (ref, c) in enumerate(((own_ref, core), (other_ref, 1 - core))):
            copies.append(pltpu.make_async_copy(ref.at[j], full.at[:, aligned(2 * j + c, feats)], sems.at[k, j]))
    for copy in copies:
        copy.start()
    return copies


def place_of(rank, core, side):
    return jnp.where(core == 0, rank, (rank % side) * side + rank // side)


def grads_kernel(side, factor, place_ref, pos_ref, rank_ref, hid_ref, own_ref, other_ref, out_ref, full, hid_t, made, sems, out_sems):
    slots, bs, _ = out_ref.shape
    col_blocks = full.shape[1] // bs
    core = place_ref[1]
    copies = join_features(core, own_ref, other_ref, full, sems)
    hid_t[...] = hid_ref[...].T
    for copy in copies:
        copy.wait()

    def out_copy(s):
        return pltpu.make_async_copy(made.at[s], out_ref.at[place_of(rank_ref[0, s], core, side)], out_sems.at[s])

    group = min(8, slots)

    def step(g, carry):
        for i in range(group):
            s = g * group + i
            p = pos_ref[0, s]
            value = jnp.dot(
                hid_t[aligned(p // col_blocks, bs), :],
                full[:, aligned(p % col_blocks, bs)],
                preferred_element_type=F32,
            )
            made[s] = (value * factor).astype(BF)
        for i in range(group):
            out_copy(g * group + i).start()
        return carry

    lax.fori_loop(0, slots // group, step, 0)

    def wait(s, carry):
        out_copy(s).wait()
        return carry

    lax.fori_loop(0, slots, wait, 0, unroll=4)


def back_kernel(place_ref, pos_ref, blocks_ref, own_ref, other_ref, out_ref, full, slab, sems):
    bs = blocks_ref.shape[1]
    copies = join_features(place_ref[1], own_ref, other_ref, full, sems)
    fill_slab(pos_ref, blocks_ref, slab)

    for copy in copies:
        copy.wait()
    value = full[...]
    step = 2 * bs
    for n in range(slab.shape[0] // step):
        rows = slab[n * step : (n + 1) * step, :]
        out_ref[:, n * step : (n + 1) * step] = lax.dot_general(
            value, rows, (((1,), (1,)), ((), ())), preferred_element_type=F32
        ).astype(BF)


def list_kernel(side, place_ref, rank_ref, in_ref, out_ref, sems):
    core = place_ref[1]
    slots = out_ref.shape[0]

    def copy(s):
        return pltpu.make_async_copy(in_ref.at[place_of(rank_ref[0, s], core, side)], out_ref.at[s], sems.at[s])

    def start(s, carry):
        copy(s).start()
        return carry

    def wait(s, carry):
        copy(s).wait()
        return carry

    lax.fori_loop(0, slots, start, 0, unroll=4)
    lax.fori_loop(0, slots, wait, 0, unroll=4)


def chip_groups(sizes):
    n0, n1, nx, nc = sizes

    def at(z, y, x, c):
        return ((z * n1 + y) * nx + x) * nc + c

    along_0 = lambda c: [[at(z, y, x, c) for z in range(n0)] for y in range(n1) for x in range(nx)]
    along_1 = lambda c: [[at(z, y, x, c) for y in range(n1)] for z in range(n0) for x in range(nx)]
    return along_0(0) + along_1(1), along_1(0) + along_0(1)


def shards(sizes, hidden, cotangent, blocks, block_pos, owner_rank, moment, second):
    tokens, feats = cotangent.shape
    rows = hidden.shape[1]
    slots, bs, _ = blocks.shape
    n0, n1, nx, nc = sizes
    width = feats * nx * nc
    axes = (*DP, *TENSOR)
    first, then = chip_groups(sizes)
    place = jnp.stack([lax.axis_index("x"), lax.axis_index("core"), lax.axis_index(DP)])
    swap = [(0, 1), (1, 0)]
    factor = 1.0 / (tokens * n0 * n1)
    block_list = jax.ShapeDtypeStruct((slots, bs, bs), BF)

    def exchange(value, groups):
        return lax.all_to_all(value, axes, 0, 0, axis_index_groups=groups, tiled=True)

    own = lax.all_to_all(jnp.broadcast_to(cotangent, (nx, tokens, feats)), "x", 0, 0, tiled=True)
    keep, send, mine = call(
        partial_kernel,
        (*(jax.ShapeDtypeStruct((nx, tokens, feats), BF),) * 2, jax.ShapeDtypeStruct((bs, bs), BF)),
        [SMEM, SMEM, SMEM, VMEM, VMEM],
        [VMEM] * 3,
        [pltpu.VMEM((rows, width), BF)],
        flops=2 * tokens * rows * width,
        nbytes=4 * 2**20,
    )(place, block_pos, owner_rank, hidden, blocks)
    own, keep, send = lax.optimization_barrier((own, keep, send))
    other = lax.ppermute(own, "core", swap)
    grads = call(
        functools.partial(grads_kernel, n0, factor),
        block_list,
        [SMEM, SMEM, SMEM, VMEM, ANY, ANY],
        ANY,
        [
            pltpu.VMEM((tokens, width), BF),
            pltpu.VMEM((rows, tokens), BF),
            pltpu.VMEM((slots, bs, bs), BF),
            pltpu.SemaphoreType.DMA((2, nx)),
            pltpu.SemaphoreType.DMA((slots,)),
        ],
        flops=2 * tokens * bs * bs * slots,
        nbytes=4 * 2**20,
        limit=12,
    )(place, block_pos, owner_rank, hidden, own, other)
    grads, keep, send = lax.optimization_barrier((grads, keep, send))
    hidden_grad = call(
        back_kernel,
        jax.ShapeDtypeStruct((tokens, rows), BF),
        [SMEM, SMEM, VMEM, ANY, ANY],
        VMEM,
        [pltpu.VMEM((tokens, width), BF), pltpu.VMEM((rows, width), BF), pltpu.SemaphoreType.DMA((2, nx))],
        flops=2 * tokens * rows * width,
        nbytes=4 * 2**20,
        limit=16,
    )(place, block_pos, blocks, own, other)

    def halved(value, step, beside=None):
        half = value.shape[0] // 2
        theirs = lax.ppermute(value[half:], "x", [(i, i ^ step) for i in range(nx)])
        theirs, beside = lax.optimization_barrier((theirs, beside))
        return (value[:half].astype(F32) + theirs.astype(F32)).astype(BF), beside

    got = exchange(grads.reshape(n0, slots // n0, bs, bs), first)
    total = (keep.astype(F32) + lax.ppermute(send, "core", swap).astype(F32)).astype(BF)
    total, hidden_grad = halved(total, 1, hidden_grad)
    got, total = lax.optimization_barrier((got, total))
    step = 2
    while total.shape[0] > 1:
        total, _ = halved(total, step)
        step *= 2
    mixed = total[0]
    part = got.astype(F32).sum(axis=0).astype(BF)
    grad = exchange(part, then).astype(F32).sum(axis=0)
    weight = mine.astype(F32)
    mom_next = 0.9 * moment[0, 0] + 0.1 * grad
    sec_next = 0.999 * second[0, 0] + 0.001 * grad * grad
    step_dir = mom_next / (jnp.sqrt(sec_next) + 1e-08)
    updated = (weight - 0.002 * (step_dir + 0.1 * weight)).astype(BF)
    row = exchange(jnp.broadcast_to(updated, (n1, bs, bs)), then)
    every = exchange(jnp.broadcast_to(row, (n0, n1, bs, bs)), first)
    new_blocks = call(
        functools.partial(list_kernel, n0),
        block_list,
        [SMEM, SMEM, ANY],
        ANY,
        [pltpu.SemaphoreType.DMA((slots,))],
        nbytes=4 * 2**20,
        limit=4,
    )(place, owner_rank, every.reshape(slots, bs, bs))
    return (mixed, hidden_grad, mom_next[None, None], sec_next[None, None], step_dir[None, None], new_blocks)


def make(sizes, torus):
    placed = (
        P(DP, TENSOR),
        P(DP, TENSOR),
        P(TENSOR, None, None),
        P(TENSOR, None),
        P(TENSOR, None),
        P(TENSOR, DP, None, None),
        P(TENSOR, DP, None, None),
    )
    return jax.shard_map(
        functools.partial(shards, sizes),
        mesh=torus,
        in_specs=placed,
        out_specs=(
            P(DP, TENSOR),
            P(DP, TENSOR),
            P(TENSOR, DP, None, None),
            P(TENSOR, DP, None, None),
            P(TENSOR, DP, None, None),
            P(TENSOR, None, None),
        ),
        check_vma=False,
    )


def solution(mesh):
    sizes = (8, mesh.shape["dp"] // 8, mesh.shape["tensor"] // 2, 2)
    return make(sizes, Mesh(mesh.devices.reshape(sizes), (*DP, *TENSOR)))
```

```python
import functools

import jax
import jax.numpy as jnp
from jax import lax
from jax.experimental import pallas as pl
from jax.experimental.pallas import tpu as pltpu
from jax.sharding import Mesh
from jax.sharding import PartitionSpec as P

DP = ("dp_0", "dp_1")
TENSOR = ("x", "core")
VMEM = pl.BlockSpec(memory_space=pltpu.VMEM)
SMEM = pl.BlockSpec(memory_space=pltpu.SMEM)
ANY = pl.BlockSpec(memory_space=pl.ANY)
BF = jnp.bfloat16
F32 = jnp.float32


def call(kernel, out_shape, ins, outs, scratch=(), flops=0, nbytes=0, limit=24):
    return pl.pallas_call(
        kernel,
        out_shape=out_shape,
        in_specs=ins,
        out_specs=outs,
        scratch_shapes=list(scratch),
        cost_estimate=pl.CostEstimate(flops=flops, bytes_accessed=nbytes, transcendentals=0),
        compiler_params=pltpu.CompilerParams(vmem_limit_bytes=limit * 2**20),
    )


def aligned(index, size):
    return pl.ds(pl.multiple_of(index * size, size), size)


def fill_slab(pos_ref, blocks_ref, slab):
    slots, bs, _ = blocks_ref.shape
    rows, width = slab.shape
    col_blocks = width // bs

    def clear(i, carry):
        slab[aligned(i, 16), :] = jnp.zeros((16, width), BF)
        return carry

    lax.fori_loop(0, rows // 16, clear, 0, unroll=2)

    def place(s, carry):
        p = pos_ref[0, s]
        slab[aligned(p // col_blocks, bs), aligned(p % col_blocks, bs)] = blocks_ref[s]
        return carry

    lax.fori_loop(0, slots, place, 0, unroll=4)


def partial_kernel(place_ref, pos_ref, rank_ref, hid_ref, blocks_ref, keep_ref, send_ref, mine_ref, hid_t_ref, slab):
    chips, _, feats = keep_ref.shape
    bits = chips.bit_length() - 1
    x, core = place_ref[0], place_ref[1]
    fill_slab(pos_ref, blocks_ref, slab)

    def find(s, found):
        return jnp.where(rank_ref[0, s] == place_ref[2], s, found)

    mine_ref[...] = blocks_ref[lax.fori_loop(0, blocks_ref.shape[0], find, 0)]
    hid = hid_ref[...]
    hid_t_ref[...] = hid.T
    for i in range(chips):
        r = sum(((i >> b) & 1) << (bits - 1 - b) for b in range(bits))
        chip = x ^ r
        for ref, c in ((keep_ref, core), (send_ref, 1 - core)):
            value = jnp.dot(hid, slab[:, aligned(2 * chip + c, feats)], preferred_element_type=F32)
            ref[i] = value.astype(BF)


def join_features(core, own_ref, other_ref, full, sems):
    pieces, _, feats = own_ref.shape
    copies = []
    for j in range(pieces):
        for k, (ref, c) in enumerate(((own_ref, core), (other_ref, 1 - core))):
            copies.append(pltpu.make_async_copy(ref.at[j], full.at[:, aligned(2 * j + c, feats)], sems.at[k, j]))
    for copy in copies:
        copy.start()
    return copies


def place_of(rank, core, side):
    return jnp.where(core == 0, rank, (rank % side) * side + rank // side)


def grads_kernel(side, factor, place_ref, pos_ref, rank_ref, hid_t, own_ref, other_ref, out_ref, full, made, sems, out_sems):
    slots, bs, _ = out_ref.shape
    col_blocks = full.shape[1] // bs
    core = place_ref[1]
    copies = join_features(core, own_ref, other_ref, full, sems)
    for copy in copies:
        copy.wait()

    def out_copy(s):
        return pltpu.make_async_copy(made.at[s], out_ref.at[place_of(rank_ref[0, s], core, side)], out_sems.at[s])

    group = min(8, slots)

    def step(g, carry):
        for i in range(group):
            s = g * group + i
            p = pos_ref[0, s]
            value = jnp.dot(
                hid_t[aligned(p // col_blocks, bs), :],
                full[:, aligned(p % col_blocks, bs)],
                preferred_element_type=F32,
            )
            made[s] = (value * factor).astype(BF)
        for i in range(group):
            out_copy(g * group + i).start()
        return carry

    lax.fori_loop(0, slots // group, step, 0)

    def wait(s, carry):
        out_copy(s).wait()
        return carry

    lax.fori_loop(0, slots, wait, 0, unroll=4)


def back_kernel(place_ref, pos_ref, blocks_ref, own_ref, other_ref, out_ref, full, slab, sems):
    bs = blocks_ref.shape[1]
    copies = join_features(place_ref[1], own_ref, other_ref, full, sems)
    fill_slab(pos_ref, blocks_ref, slab)

    for copy in copies:
        copy.wait()
    value = full[...]
    step = 2 * bs
    for n in range(slab.shape[0] // step):
        rows = slab[n * step : (n + 1) * step, :]
        out_ref[:, n * step : (n + 1) * step] = lax.dot_general(
            value, rows, (((1,), (1,)), ((), ())), preferred_element_type=F32
        ).astype(BF)


def list_kernel(side, place_ref, rank_ref, in_ref, out_ref, sems):
    core = place_ref[1]
    slots = out_ref.shape[0]

    def copy(s):
        return pltpu.make_async_copy(in_ref.at[place_of(rank_ref[0, s], core, side)], out_ref.at[s], sems.at[s])

    for s in range(slots):
        copy(s).start()
    for s in range(slots):
        copy(s).wait()


def chip_groups(sizes):
    n0, n1, nx, nc = sizes

    def at(z, y, x, c):
        return ((z * n1 + y) * nx + x) * nc + c

    along_0 = lambda c: [[at(z, y, x, c) for z in range(n0)] for y in range(n1) for x in range(nx)]
    along_1 = lambda c: [[at(z, y, x, c) for y in range(n1)] for z in range(n0) for x in range(nx)]
    return along_0(0) + along_1(1), along_1(0) + along_0(1)


def shards(sizes, hidden, cotangent, blocks, block_pos, owner_rank, moment, second):
    tokens, feats = cotangent.shape
    rows = hidden.shape[1]
    slots, bs, _ = blocks.shape
    n0, n1, nx, nc = sizes
    width = feats * nx * nc
    axes = (*DP, *TENSOR)
    first, then = chip_groups(sizes)
    place = jnp.stack([lax.axis_index("x"), lax.axis_index("core"), lax.axis_index(DP)])
    swap = [(0, 1), (1, 0)]
    factor = 1.0 / (tokens * n0 * n1)
    block_list = jax.ShapeDtypeStruct((slots, bs, bs), BF)

    def exchange(value, groups):
        return lax.all_to_all(value, axes, 0, 0, axis_index_groups=groups, tiled=True)

    own = lax.all_to_all(jnp.broadcast_to(cotangent, (nx, tokens, feats)), "x", 0, 0, tiled=True)
    keep, send, mine, hid_t = call(
        partial_kernel,
        (*(jax.ShapeDtypeStruct((nx, tokens, feats), BF),) * 2, jax.ShapeDtypeStruct((bs, bs), BF), jax.ShapeDtypeStruct((rows, tokens), BF)),
        [SMEM, SMEM, SMEM, VMEM, VMEM],
        [VMEM] * 4,
        [pltpu.VMEM((rows, width), BF)],
        flops=2 * tokens * rows * width,
        nbytes=4 * 2**20,
    )(place, block_pos, owner_rank, hidden, blocks)
    own, keep, send = lax.optimization_barrier((own, keep, send))
    other = lax.ppermute(own, "core", swap)
    grads = call(
        functools.partial(grads_kernel, n0, factor),
        block_list,
        [SMEM, SMEM, SMEM, VMEM, ANY, ANY],
        ANY,
        [
            pltpu.VMEM((tokens, width), BF),
            pltpu.VMEM((slots, bs, bs), BF),
            pltpu.SemaphoreType.DMA((2, nx)),
            pltpu.SemaphoreType.DMA((slots,)),
        ],
        flops=2 * tokens * bs * bs * slots,
        nbytes=4 * 2**20,
        limit=12,
    )(place, block_pos, owner_rank, hid_t, own, other)
    grads, keep, send = lax.optimization_barrier((grads, keep, send))
    hidden_grad = call(
        back_kernel,
        jax.ShapeDtypeStruct((tokens, rows), BF),
        [SMEM, SMEM, VMEM, ANY, ANY],
        VMEM,
        [pltpu.VMEM((tokens, width), BF), pltpu.VMEM((rows, width), BF), pltpu.SemaphoreType.DMA((2, nx))],
        flops=2 * tokens * rows * width,
        nbytes=4 * 2**20,
        limit=16,
    )(place, block_pos, blocks, own, other)

    def halved(value, step, beside=None):
        half = value.shape[0] // 2
        theirs = lax.ppermute(value[half:], "x", [(i, i ^ step) for i in range(nx)])
        theirs, beside = lax.optimization_barrier((theirs, beside))
        return (value[:half].astype(F32) + theirs.astype(F32)).astype(BF), beside

    got = exchange(grads.reshape(n0, slots // n0, bs, bs), first)
    total = (keep.astype(F32) + lax.ppermute(send, "core", swap).astype(F32)).astype(BF)
    total, hidden_grad = halved(total, 1, hidden_grad)
    part = got.astype(F32).sum(axis=0).astype(BF)
    part, total = lax.optimization_barrier((part, total))
    step = 2
    while total.shape[0] > 1:
        total, _ = halved(total, step)
        step *= 2
    mixed = total[0]
    grad = exchange(part, then).astype(F32).sum(axis=0)
    weight = mine.astype(F32)
    mom_next = 0.9 * moment[0, 0] + 0.1 * grad
    sec_next = 0.999 * second[0, 0] + 0.001 * grad * grad
    step_dir = mom_next / (jnp.sqrt(sec_next) + 1e-08)
    updated = (weight - 0.002 * (step_dir + 0.1 * weight)).astype(BF)
    row = exchange(jnp.broadcast_to(updated, (n1, bs, bs)), then)
    every = exchange(jnp.broadcast_to(row, (n0, n1, bs, bs)), first)
    new_blocks = call(
        functools.partial(list_kernel, n0),
        block_list,
        [SMEM, SMEM, ANY],
        ANY,
        [pltpu.SemaphoreType.DMA((slots,))],
        nbytes=4 * 2**20,
        limit=4,
    )(place, owner_rank, every.reshape(slots, bs, bs))
    return (mixed, hidden_grad, mom_next[None, None], sec_next[None, None], step_dir[None, None], new_blocks)


def make(sizes, torus):
    placed = (
        P(DP, TENSOR),
        P(DP, TENSOR),
        P(TENSOR, None, None),
        P(TENSOR, None),
        P(TENSOR, None),
        P(TENSOR, DP, None, None),
        P(TENSOR, DP, None, None),
    )
    return jax.shard_map(
        functools.partial(shards, sizes),
        mesh=torus,
        in_specs=placed,
        out_specs=(
            P(DP, TENSOR),
            P(DP, TENSOR),
            P(TENSOR, DP, None, None),
            P(TENSOR, DP, None, None),
            P(TENSOR, DP, None, None),
            P(TENSOR, None, None),
        ),
        check_vma=False,
    )


def solution(mesh):
    sizes = (8, mesh.shape["dp"] // 8, mesh.shape["tensor"] // 2, 2)
    return make(sizes, Mesh(mesh.devices.reshape(sizes), (*DP, *TENSOR)))
```

```python
import functools

import jax
import jax.numpy as jnp
from jax import lax
from jax.experimental import pallas as pl
from jax.experimental.pallas import tpu as pltpu
from jax.sharding import Mesh
from jax.sharding import PartitionSpec as P

DP = ("dp_0", "dp_1")
TENSOR = ("x", "core")
VMEM = pl.BlockSpec(memory_space=pltpu.VMEM)
SMEM = pl.BlockSpec(memory_space=pltpu.SMEM)
ANY = pl.BlockSpec(memory_space=pl.ANY)
BF = jnp.bfloat16
F32 = jnp.float32
SHIFTS = (0, 5, 2, 6, 1, 7, 4, 3)


def call(kernel, out_shape, ins, outs, scratch=(), flops=0, nbytes=0, limit=24):
    return pl.pallas_call(
        kernel,
        out_shape=out_shape,
        in_specs=ins,
        out_specs=outs,
        scratch_shapes=list(scratch),
        cost_estimate=pl.CostEstimate(flops=flops, bytes_accessed=nbytes, transcendentals=0),
        compiler_params=pltpu.CompilerParams(vmem_limit_bytes=limit * 2**20),
    )


def aligned(index, size):
    return pl.ds(pl.multiple_of(index * size, size), size)


def fill_slab(pos_ref, blocks_ref, slab):
    slots, bs, _ = blocks_ref.shape
    rows, width = slab.shape
    col_blocks = width // bs

    def clear(i, carry):
        slab[aligned(i, 16), :] = jnp.zeros((16, width), BF)
        return carry

    lax.fori_loop(0, rows // 16, clear, 0, unroll=2)

    def place(s, carry):
        p = pos_ref[0, s]
        slab[aligned(p // col_blocks, bs), aligned(p % col_blocks, bs)] = blocks_ref[s]
        return carry

    lax.fori_loop(0, slots, place, 0, unroll=4)


def partial_kernel(place_ref, pos_ref, rank_ref, hid_ref, blocks_ref, keep_ref, send_ref, mine_ref, hid_t_ref, slab):
    chips, _, feats = keep_ref.shape
    bits = chips.bit_length() - 1
    x, core = place_ref[0], place_ref[1]
    fill_slab(pos_ref, blocks_ref, slab)

    def find(s, found):
        return jnp.where(rank_ref[0, s] == place_ref[2], s, found)

    mine_ref[...] = blocks_ref[lax.fori_loop(0, blocks_ref.shape[0], find, 0)]
    hid = hid_ref[...]
    hid_t_ref[...] = hid.T
    for i in range(chips):
        r = sum(((i >> b) & 1) << (bits - 1 - b) for b in range(bits))
        chip = x ^ r
        for ref, c in ((keep_ref, core), (send_ref, 1 - core)):
            value = jnp.dot(hid, slab[:, aligned(2 * chip + c, feats)], preferred_element_type=F32)
            ref[i] = value.astype(BF)


def join_features(core, own_ref, other_ref, full, sems):
    pieces, _, feats = own_ref.shape
    copies = []
    for j in range(pieces):
        for k, (ref, c) in enumerate(((own_ref, core), (other_ref, 1 - core))):
            copies.append(pltpu.make_async_copy(ref.at[j], full.at[:, aligned(2 * j + c, feats)], sems.at[k, j]))
    for copy in copies:
        copy.start()
    return copies


def place_of(rank, core, side):
    return jnp.where(core == 0, rank, (rank % side) * side + rank // side)


def grads_kernel(side, factor, place_ref, pos_ref, rank_ref, hid_t, own_ref, other_ref, out_ref, full, made, sems, out_sems):
    slots, bs, _ = out_ref.shape
    col_blocks = full.shape[1] // bs
    core = place_ref[1]
    copies = join_features(core, own_ref, other_ref, full, sems)
    for copy in copies:
        copy.wait()

    def out_copy(s):
        return pltpu.make_async_copy(made.at[s], out_ref.at[place_of(rank_ref[0, s], core, side)], out_sems.at[s])

    group = min(8, slots)

    def step(g, carry):
        for i in range(group):
            s = g * group + i
            p = pos_ref[0, s]
            value = jnp.dot(
                hid_t[aligned(p // col_blocks, bs), :],
                full[:, aligned(p % col_blocks, bs)],
                preferred_element_type=F32,
            )
            made[s] = (value * factor).astype(BF)
        for i in range(group):
            out_copy(g * group + i).start()
        return carry

    lax.fori_loop(0, slots // group, step, 0)

    def wait(s, carry):
        out_copy(s).wait()
        return carry

    lax.fori_loop(0, slots, wait, 0, unroll=4)


def back_kernel(place_ref, pos_ref, blocks_ref, own_ref, other_ref, out_ref, full, slab, sems):
    bs = blocks_ref.shape[1]
    copies = join_features(place_ref[1], own_ref, other_ref, full, sems)
    fill_slab(pos_ref, blocks_ref, slab)

    for copy in copies:
        copy.wait()
    value = full[...]
    step = 2 * bs
    for n in range(slab.shape[0] // step):
        rows = slab[n * step : (n + 1) * step, :]
        out_ref[:, n * step : (n + 1) * step] = lax.dot_general(
            value, rows, (((1,), (1,)), ((), ())), preferred_element_type=F32
        ).astype(BF)


def list_kernel(side, shifts, place_ref, rank_ref, *refs):
    rows, (out_ref, slot_of, sems) = refs[:-3], refs[-3:]
    core, along = place_ref[1], place_ref[3]
    for s in range(out_ref.shape[0]):
        slot_of[rank_ref[0, s]] = s
    copies = []
    for k, row_ref in enumerate(rows):
        j = (along + side - shifts[k]) % side
        for i in range(row_ref.shape[0]):
            rank = jnp.where(core == 0, j * side + i, i * side + j)
            copies.append(pltpu.make_async_copy(row_ref.at[i], out_ref.at[slot_of[rank]], sems.at[k, i]))
    for copy in copies:
        copy.start()
    for copy in copies:
        copy.wait()


def chip_groups(sizes):
    n0, n1, nx, nc = sizes

    def at(z, y, x, c):
        return ((z * n1 + y) * nx + x) * nc + c

    along_0 = lambda c: [[at(z, y, x, c) for z in range(n0)] for y in range(n1) for x in range(nx)]
    along_1 = lambda c: [[at(z, y, x, c) for y in range(n1)] for z in range(n0) for x in range(nx)]
    return along_0(0) + along_1(1), along_1(0) + along_0(1)


def ring_shift(sizes, k):
    n0, n1, nx, nc = sizes
    pairs = []
    for z in range(n0):
        for y in range(n1):
            to = ((z + k) % n0, y), (z, (y + k) % n1)
            for x in range(nx):
                for c in range(nc):
                    there = (to[c][0] * n1 + to[c][1]) * nx + x
                    pairs.append((((z * n1 + y) * nx + x) * nc + c, there * nc + c))
    return pairs


def shards(sizes, hidden, cotangent, blocks, block_pos, owner_rank, moment, second):
    tokens, feats = cotangent.shape
    rows = hidden.shape[1]
    slots, bs, _ = blocks.shape
    n0, n1, nx, nc = sizes
    width = feats * nx * nc
    axes = (*DP, *TENSOR)
    first, then = chip_groups(sizes)
    along = jnp.where(lax.axis_index("core") == 0, lax.axis_index(DP[0]), lax.axis_index(DP[1]))
    place = jnp.stack([lax.axis_index("x"), lax.axis_index("core"), lax.axis_index(DP), along])
    swap = [(0, 1), (1, 0)]
    factor = 1.0 / (tokens * n0 * n1)
    block_list = jax.ShapeDtypeStruct((slots, bs, bs), BF)

    def exchange(value, groups):
        return lax.all_to_all(value, axes, 0, 0, axis_index_groups=groups, tiled=True)

    own = lax.all_to_all(jnp.broadcast_to(cotangent, (nx, tokens, feats)), "x", 0, 0, tiled=True)
    keep, send, mine, hid_t = call(
        partial_kernel,
        (*(jax.ShapeDtypeStruct((nx, tokens, feats), BF),) * 2, jax.ShapeDtypeStruct((bs, bs), BF), jax.ShapeDtypeStruct((rows, tokens), BF)),
        [SMEM, SMEM, SMEM, VMEM, VMEM],
        [VMEM] * 4,
        [pltpu.VMEM((rows, width), BF)],
        flops=2 * tokens * rows * width,
        nbytes=4 * 2**20,
    )(place, block_pos, owner_rank, hidden, blocks)
    own, keep, send = lax.optimization_barrier((own, keep, send))
    other = lax.ppermute(own, "core", swap)
    grads = call(
        functools.partial(grads_kernel, n0, factor),
        block_list,
        [SMEM, SMEM, SMEM, VMEM, ANY, ANY],
        ANY,
        [
            pltpu.VMEM((tokens, width), BF),
            pltpu.VMEM((slots, bs, bs), BF),
            pltpu.SemaphoreType.DMA((2, nx)),
            pltpu.SemaphoreType.DMA((slots,)),
        ],
        flops=2 * tokens * bs * bs * slots,
        nbytes=4 * 2**20,
        limit=12,
    )(place, block_pos, owner_rank, hid_t, own, other)
    grads, keep, send = lax.optimization_barrier((grads, keep, send))
    hidden_grad = call(
        back_kernel,
        jax.ShapeDtypeStruct((tokens, rows), BF),
        [SMEM, SMEM, VMEM, ANY, ANY],
        VMEM,
        [pltpu.VMEM((tokens, width), BF), pltpu.VMEM((rows, width), BF), pltpu.SemaphoreType.DMA((2, nx))],
        flops=2 * tokens * rows * width,
        nbytes=4 * 2**20,
        limit=16,
    )(place, block_pos, blocks, own, other)

    def halved(value, step, beside=None):
        half = value.shape[0] // 2
        theirs = lax.ppermute(value[half:], "x", [(i, i ^ step) for i in range(nx)])
        theirs, beside = lax.optimization_barrier((theirs, beside))
        return (value[:half].astype(F32) + theirs.astype(F32)).astype(BF), beside

    got = exchange(grads.reshape(n0, slots // n0, bs, bs), first)
    total = (keep.astype(F32) + lax.ppermute(send, "core", swap).astype(F32)).astype(BF)
    total, hidden_grad = halved(total, 1, hidden_grad)
    if total.shape[0] > 1:
        total, _ = halved(total, 2)
    part = got.astype(F32).sum(axis=0).astype(BF)
    part, total = lax.optimization_barrier((part, total))
    grad = exchange(part, then).astype(F32).sum(axis=0)
    weight = mine.astype(F32)
    mom_next = 0.9 * moment[0, 0] + 0.1 * grad
    sec_next = 0.999 * second[0, 0] + 0.001 * grad * grad
    step_dir = mom_next / (jnp.sqrt(sec_next) + 1e-08)
    updated = (weight - 0.002 * (step_dir + 0.1 * weight)).astype(BF)
    row = exchange(jnp.broadcast_to(updated, (n1, bs, bs)), then)
    row, total = lax.optimization_barrier((row, total))
    step = 4
    while total.shape[0] > 1:
        total, _ = halved(total, step)
        step *= 2
    mixed = total[0]
    shifts = SHIFTS if n0 == len(SHIFTS) else tuple(range(n0))
    rows_from = [lax.ppermute(row, axes, ring_shift(sizes, k)) if k else row for k in shifts]
    new_blocks = call(
        functools.partial(list_kernel, n0, shifts),
        block_list,
        [SMEM, SMEM] + [ANY] * n0,
        ANY,
        [pltpu.SMEM((slots,), jnp.int32), pltpu.SemaphoreType.DMA((n0, slots // n0))],
        nbytes=4 * 2**20,
        limit=4,
    )(place, owner_rank, *rows_from)
    return (mixed, hidden_grad, mom_next[None, None], sec_next[None, None], step_dir[None, None], new_blocks)


def make(sizes, torus):
    placed = (
        P(DP, TENSOR),
        P(DP, TENSOR),
        P(TENSOR, None, None),
        P(TENSOR, None),
        P(TENSOR, None),
        P(TENSOR, DP, None, None),
        P(TENSOR, DP, None, None),
    )
    return jax.shard_map(
        functools.partial(shards, sizes),
        mesh=torus,
        in_specs=placed,
        out_specs=(
            P(DP, TENSOR),
            P(DP, TENSOR),
            P(TENSOR, DP, None, None),
            P(TENSOR, DP, None, None),
            P(TENSOR, DP, None, None),
            P(TENSOR, None, None),
        ),
        check_vma=False,
    )


def solution(mesh):
    sizes = (8, mesh.shape["dp"] // 8, mesh.shape["tensor"] // 2, 2)
    step = make(sizes, Mesh(mesh.devices.reshape(sizes), (*DP, *TENSOR)))
    return step
```

```python
import functools

import jax
import jax.numpy as jnp
from jax import lax
from jax.experimental import pallas as pl
from jax.experimental.pallas import tpu as pltpu
from jax.sharding import Mesh
from jax.sharding import PartitionSpec as P

DP = ("dp_0", "dp_1")
TENSOR = ("x", "core")
VMEM = pl.BlockSpec(memory_space=pltpu.VMEM)
SMEM = pl.BlockSpec(memory_space=pltpu.SMEM)
ANY = pl.BlockSpec(memory_space=pl.ANY)
BF = jnp.bfloat16
F32 = jnp.float32
SHIFTS = (0, 5, 2, 6, 1, 7, 4, 3)


def call(kernel, out_shape, ins, outs, scratch=(), flops=0, nbytes=0, limit=24):
    return pl.pallas_call(
        kernel,
        out_shape=out_shape,
        in_specs=ins,
        out_specs=outs,
        scratch_shapes=list(scratch),
        cost_estimate=pl.CostEstimate(flops=flops, bytes_accessed=nbytes, transcendentals=0),
        compiler_params=pltpu.CompilerParams(vmem_limit_bytes=limit * 2**20),
    )


def aligned(index, size):
    return pl.ds(pl.multiple_of(index * size, size), size)


def fill_slab(pos_ref, blocks_ref, slab):
    slots, bs, _ = blocks_ref.shape
    rows, width = slab.shape
    col_blocks = width // bs

    def clear(i, carry):
        slab[aligned(i, 16), :] = jnp.zeros((16, width), BF)
        return carry

    lax.fori_loop(0, rows // 16, clear, 0, unroll=2)

    def place(s, carry):
        p = pos_ref[0, s]
        slab[aligned(p // col_blocks, bs), aligned(p % col_blocks, bs)] = blocks_ref[s]
        return carry

    lax.fori_loop(0, slots, place, 0, unroll=4)


def partial_kernel(place_ref, pos_ref, rank_ref, hid_ref, blocks_ref, keep_ref, send_ref, mine_ref, hid_t_ref, slab):
    chips, _, feats = keep_ref.shape
    bits = chips.bit_length() - 1
    x, core = place_ref[0], place_ref[1]
    fill_slab(pos_ref, blocks_ref, slab)

    def find(s, found):
        return jnp.where(rank_ref[0, s] == place_ref[2], s, found)

    mine_ref[...] = blocks_ref[lax.fori_loop(0, blocks_ref.shape[0], find, 0)]
    hid = hid_ref[...]
    hid_t_ref[...] = hid.T
    for i in range(chips):
        r = sum(((i >> b) & 1) << (bits - 1 - b) for b in range(bits))
        chip = x ^ r
        for ref, c in ((keep_ref, core), (send_ref, 1 - core)):
            value = jnp.dot(hid, slab[:, aligned(2 * chip + c, feats)], preferred_element_type=F32)
            ref[i] = value.astype(BF)


def join_features(core, own_ref, other_ref, full, sems):
    pieces, _, feats = own_ref.shape
    copies = []
    for j in range(pieces):
        for k, (ref, c) in enumerate(((own_ref, core), (other_ref, 1 - core))):
            copies.append(pltpu.make_async_copy(ref.at[j], full.at[:, aligned(2 * j + c, feats)], sems.at[k, j]))
    for copy in copies:
        copy.start()
    return copies


def place_of(rank, core, side):
    return jnp.where(core == 0, rank, (rank % side) * side + rank // side)


def grads_kernel(side, factor, place_ref, pos_ref, rank_ref, hid_t, own_ref, other_ref, out_ref, full, made, sems, out_sems):
    slots, bs, _ = out_ref.shape
    col_blocks = full.shape[1] // bs
    core = place_ref[1]
    copies = join_features(core, own_ref, other_ref, full, sems)
    for copy in copies:
        copy.wait()

    def out_copy(s):
        return pltpu.make_async_copy(made.at[s], out_ref.at[place_of(rank_ref[0, s], core, side)], out_sems.at[s])

    group = min(8, slots)

    def step(g, carry):
        for i in range(group):
            s = g * group + i
            p = pos_ref[0, s]
            value = jnp.dot(
                hid_t[aligned(p // col_blocks, bs), :],
                full[:, aligned(p % col_blocks, bs)],
                preferred_element_type=F32,
            )
            made[s] = (value * factor).astype(BF)
        for i in range(group):
            out_copy(g * group + i).start()
        return carry

    lax.fori_loop(0, slots // group, step, 0)

    def wait(s, carry):
        out_copy(s).wait()
        return carry

    lax.fori_loop(0, slots, wait, 0, unroll=4)


def back_kernel(place_ref, pos_ref, blocks_ref, own_ref, other_ref, out_ref, full, slab, sems):
    bs = blocks_ref.shape[1]
    copies = join_features(place_ref[1], own_ref, other_ref, full, sems)
    fill_slab(pos_ref, blocks_ref, slab)

    for copy in copies:
        copy.wait()
    value = full[...]
    step = 2 * bs
    for n in range(slab.shape[0] // step):
        rows = slab[n * step : (n + 1) * step, :]
        out_ref[:, n * step : (n + 1) * step] = lax.dot_general(
            value, rows, (((1,), (1,)), ((), ())), preferred_element_type=F32
        ).astype(BF)


def list_kernel(side, shifts, place_ref, rank_ref, *refs):
    rows, (out_ref, slot_of, sems) = refs[:-3], refs[-3:]
    core, along = place_ref[1], place_ref[3]
    for s in range(out_ref.shape[0]):
        slot_of[rank_ref[0, s]] = s
    copies = []
    for k, row_ref in enumerate(rows):
        j = (along + side - shifts[k]) % side
        for i in range(row_ref.shape[0]):
            rank = jnp.where(core == 0, j * side + i, i * side + j)
            copies.append(pltpu.make_async_copy(row_ref.at[i], out_ref.at[slot_of[rank]], sems.at[k, i]))
    for copy in copies:
        copy.start()
    for copy in copies:
        copy.wait()


def chip_groups(sizes):
    n0, n1, nx, nc = sizes

    def at(z, y, x, c):
        return ((z * n1 + y) * nx + x) * nc + c

    along_0 = lambda c: [[at(z, y, x, c) for z in range(n0)] for y in range(n1) for x in range(nx)]
    along_1 = lambda c: [[at(z, y, x, c) for y in range(n1)] for z in range(n0) for x in range(nx)]
    return along_0(0) + along_1(1), along_1(0) + along_0(1)


def ring_shift(sizes, k):
    n0, n1, nx, nc = sizes
    pairs = []
    for z in range(n0):
        for y in range(n1):
            to = ((z + k) % n0, y), (z, (y + k) % n1)
            for x in range(nx):
                for c in range(nc):
                    there = (to[c][0] * n1 + to[c][1]) * nx + x
                    pairs.append((((z * n1 + y) * nx + x) * nc + c, there * nc + c))
    return pairs


def shards(sizes, hidden, cotangent, blocks, block_pos, owner_rank, moment, second):
    tokens, feats = cotangent.shape
    rows = hidden.shape[1]
    slots, bs, _ = blocks.shape
    n0, n1, nx, nc = sizes
    width = feats * nx * nc
    axes = (*DP, *TENSOR)
    first, then = chip_groups(sizes)
    along = jnp.where(lax.axis_index("core") == 0, lax.axis_index(DP[0]), lax.axis_index(DP[1]))
    place = jnp.stack([lax.axis_index("x"), lax.axis_index("core"), lax.axis_index(DP), along])
    swap = [(0, 1), (1, 0)]
    factor = 1.0 / (tokens * n0 * n1)
    block_list = jax.ShapeDtypeStruct((slots, bs, bs), BF)

    def exchange(value, groups):
        return lax.all_to_all(value, axes, 0, 0, axis_index_groups=groups, tiled=True)

    own = lax.all_to_all(jnp.broadcast_to(cotangent, (nx, tokens, feats)), "x", 0, 0, tiled=True)
    keep, send, mine, hid_t = call(
        partial_kernel,
        (*(jax.ShapeDtypeStruct((nx, tokens, feats), BF),) * 2, jax.ShapeDtypeStruct((bs, bs), BF), jax.ShapeDtypeStruct((rows, tokens), BF)),
        [SMEM, SMEM, SMEM, VMEM, VMEM],
        [VMEM] * 4,
        [pltpu.VMEM((rows, width), BF)],
        flops=2 * tokens * rows * width,
        nbytes=4 * 2**20,
        limit=60,
    )(place, block_pos, owner_rank, hidden, blocks)
    swapped = lax.ppermute(send, "core", swap)
    own, keep, swapped = lax.optimization_barrier((own, keep, swapped))
    other = lax.ppermute(own, "core", swap)
    grads = call(
        functools.partial(grads_kernel, n0, factor),
        block_list,
        [SMEM, SMEM, SMEM, VMEM, ANY, ANY],
        ANY,
        [
            pltpu.VMEM((tokens, width), BF),
            pltpu.VMEM((slots, bs, bs), BF),
            pltpu.SemaphoreType.DMA((2, nx)),
            pltpu.SemaphoreType.DMA((slots,)),
        ],
        flops=2 * tokens * bs * bs * slots,
        nbytes=4 * 2**20,
        limit=12,
    )(place, block_pos, owner_rank, hid_t, own, other)
    grads, keep, swapped = lax.optimization_barrier((grads, keep, swapped))
    hidden_grad = call(
        back_kernel,
        jax.ShapeDtypeStruct((tokens, rows), BF),
        [SMEM, SMEM, VMEM, ANY, ANY],
        VMEM,
        [pltpu.VMEM((tokens, width), BF), pltpu.VMEM((rows, width), BF), pltpu.SemaphoreType.DMA((2, nx))],
        flops=2 * tokens * rows * width,
        nbytes=4 * 2**20,
        limit=16,
    )(place, block_pos, blocks, own, other)

    def halved(value, step, beside=None):
        half = value.shape[0] // 2
        theirs = lax.ppermute(value[half:], "x", [(i, i ^ step) for i in range(nx)])
        theirs, beside = lax.optimization_barrier((theirs, beside))
        return (value[:half].astype(F32) + theirs.astype(F32)).astype(BF), beside

    got = exchange(grads.reshape(n0, slots // n0, bs, bs), first)
    total = (keep.astype(F32) + swapped.astype(F32)).astype(BF)
    total, hidden_grad = halved(total, 1, hidden_grad)
    if total.shape[0] > 1:
        total, _ = halved(total, 2)
    part = got.astype(F32).sum(axis=0).astype(BF)
    part, total = lax.optimization_barrier((part, total))
    grad = exchange(part, then).astype(F32).sum(axis=0)
    weight = mine.astype(F32)
    mom_next = 0.9 * moment[0, 0] + 0.1 * grad
    sec_next = 0.999 * second[0, 0] + 0.001 * grad * grad
    step_dir = mom_next / (jnp.sqrt(sec_next) + 1e-08)
    updated = (weight - 0.002 * (step_dir + 0.1 * weight)).astype(BF)
    row = exchange(jnp.broadcast_to(updated, (n1, bs, bs)), then)
    row, total = lax.optimization_barrier((row, total))
    step = 4
    while total.shape[0] > 1:
        total, _ = halved(total, step)
        step *= 2
    mixed = total[0]
    shifts = SHIFTS if n0 == len(SHIFTS) else tuple(range(n0))
    rows_from = [lax.ppermute(row, axes, ring_shift(sizes, k)) if k else row for k in shifts]
    new_blocks = call(
        functools.partial(list_kernel, n0, shifts),
        block_list,
        [SMEM, SMEM] + [ANY] * n0,
        ANY,
        [pltpu.SMEM((slots,), jnp.int32), pltpu.SemaphoreType.DMA((n0, slots // n0))],
        nbytes=4 * 2**20,
        limit=4,
    )(place, owner_rank, *rows_from)
    return (mixed, hidden_grad, mom_next[None, None], sec_next[None, None], step_dir[None, None], new_blocks)


def make(sizes, torus):
    placed = (
        P(DP, TENSOR),
        P(DP, TENSOR),
        P(TENSOR, None, None),
        P(TENSOR, None),
        P(TENSOR, None),
        P(TENSOR, DP, None, None),
        P(TENSOR, DP, None, None),
    )
    return jax.shard_map(
        functools.partial(shards, sizes),
        mesh=torus,
        in_specs=placed,
        out_specs=(
            P(DP, TENSOR),
            P(DP, TENSOR),
            P(TENSOR, DP, None, None),
            P(TENSOR, DP, None, None),
            P(TENSOR, DP, None, None),
            P(TENSOR, None, None),
        ),
        check_vma=False,
    )


def solution(mesh):
    sizes = (8, mesh.shape["dp"] // 8, mesh.shape["tensor"] // 2, 2)
    step = make(sizes, Mesh(mesh.devices.reshape(sizes), (*DP, *TENSOR)))
    return step
```

```python
import functools

import jax
import jax.numpy as jnp
from jax import lax
from jax.experimental import pallas as pl
from jax.experimental.pallas import tpu as pltpu
from jax.sharding import Mesh
from jax.sharding import PartitionSpec as P

DP = ("dp_0", "dp_1")
TENSOR = ("x", "core")
VMEM = pl.BlockSpec(memory_space=pltpu.VMEM)
SMEM = pl.BlockSpec(memory_space=pltpu.SMEM)
ANY = pl.BlockSpec(memory_space=pl.ANY)
BF = jnp.bfloat16
F32 = jnp.float32


def call(kernel, out_shape, ins, outs, scratch=(), flops=0, nbytes=0, limit=24):
    return pl.pallas_call(
        kernel,
        out_shape=out_shape,
        in_specs=ins,
        out_specs=outs,
        scratch_shapes=list(scratch),
        cost_estimate=pl.CostEstimate(flops=flops, bytes_accessed=nbytes, transcendentals=0),
        compiler_params=pltpu.CompilerParams(vmem_limit_bytes=limit * 2**20),
    )


def aligned(index, size):
    return pl.ds(pl.multiple_of(index * size, size), size)


def fill_slab(pos_ref, blocks_ref, slab):
    slots, bs, _ = blocks_ref.shape
    rows, width = slab.shape
    col_blocks = width // bs

    def clear(i, carry):
        slab[aligned(i, 16), :] = jnp.zeros((16, width), BF)
        return carry

    lax.fori_loop(0, rows // 16, clear, 0, unroll=2)

    def place(s, carry):
        p = pos_ref[0, s]
        slab[aligned(p // col_blocks, bs), aligned(p % col_blocks, bs)] = blocks_ref[s]
        return carry

    lax.fori_loop(0, slots, place, 0, unroll=4)


def partial_kernel(place_ref, pos_ref, rank_ref, hid_ref, blocks_ref, keep_ref, send_ref, mine_ref, hid_t_ref, slab):
    chips, _, feats = keep_ref.shape
    bits = chips.bit_length() - 1
    x, core = place_ref[0], place_ref[1]
    fill_slab(pos_ref, blocks_ref, slab)

    def find(s, found):
        return jnp.where(rank_ref[0, s] == place_ref[2], s, found)

    mine_ref[...] = blocks_ref[lax.fori_loop(0, blocks_ref.shape[0], find, 0)]
    hid = hid_ref[...]
    hid_t_ref[...] = hid.T
    for i in range(chips):
        r = sum(((i >> b) & 1) << (bits - 1 - b) for b in range(bits))
        chip = x ^ r
        for ref, c in ((keep_ref, core), (send_ref, 1 - core)):
            value = jnp.dot(hid, slab[:, aligned(2 * chip + c, feats)], preferred_element_type=F32)
            ref[i] = value.astype(BF)


def join_features(core, own_ref, other_ref, full, sems):
    pieces, _, feats = own_ref.shape
    copies = []
    for j in range(pieces):
        for k, (ref, c) in enumerate(((own_ref, core), (other_ref, 1 - core))):
            copies.append(pltpu.make_async_copy(ref.at[j], full.at[:, aligned(2 * j + c, feats)], sems.at[k, j]))
    for copy in copies:
        copy.start()
    return copies


def place_of(rank, core, side):
    return jnp.where(core == 0, rank, (rank % side) * side + rank // side)


def grads_kernel(side, factor, place_ref, pos_ref, rank_ref, hid_t, own_ref, other_ref, out_ref, full, made, sems, out_sems):
    slots, bs, _ = out_ref.shape
    col_blocks = full.shape[1] // bs
    core = place_ref[1]
    copies = join_features(core, own_ref, other_ref, full, sems)
    for copy in copies:
        copy.wait()

    def out_copy(s):
        return pltpu.make_async_copy(made.at[s], out_ref.at[place_of(rank_ref[0, s], core, side)], out_sems.at[s])

    group = min(8, slots)

    def step(g, carry):
        for i in range(group):
            s = g * group + i
            p = pos_ref[0, s]
            value = jnp.dot(
                hid_t[aligned(p // col_blocks, bs), :],
                full[:, aligned(p % col_blocks, bs)],
                preferred_element_type=F32,
            )
            made[s] = (value * factor).astype(BF)
        for i in range(group):
            out_copy(g * group + i).start()
        return carry

    lax.fori_loop(0, slots // group, step, 0)

    def wait(s, carry):
        out_copy(s).wait()
        return carry

    lax.fori_loop(0, slots, wait, 0, unroll=4)


def back_kernel(place_ref, pos_ref, blocks_ref, own_ref, other_ref, out_ref, full, slab, sems):
    bs = blocks_ref.shape[1]
    copies = join_features(place_ref[1], own_ref, other_ref, full, sems)
    fill_slab(pos_ref, blocks_ref, slab)

    for copy in copies:
        copy.wait()
    value = full[...]
    step = 2 * bs
    for n in range(slab.shape[0] // step):
        rows = slab[n * step : (n + 1) * step, :]
        out_ref[:, n * step : (n + 1) * step] = lax.dot_general(
            value, rows, (((1,), (1,)), ((), ())), preferred_element_type=F32
        ).astype(BF)


def list_kernel(side, place_ref, rank_ref, in_ref, out_ref, sems):
    core = place_ref[1]
    slots = out_ref.shape[0]

    def copy(s):
        return pltpu.make_async_copy(in_ref.at[place_of(rank_ref[0, s], core, side)], out_ref.at[s], sems.at[s])

    for s in range(slots):
        copy(s).start()
    for s in range(slots):
        copy(s).wait()


def chip_groups(sizes):
    n0, n1, nx, nc = sizes

    def at(z, y, x, c):
        return ((z * n1 + y) * nx + x) * nc + c

    along_0 = lambda c: [[at(z, y, x, c) for z in range(n0)] for y in range(n1) for x in range(nx)]
    along_1 = lambda c: [[at(z, y, x, c) for y in range(n1)] for z in range(n0) for x in range(nx)]
    return along_0(0) + along_1(1), along_1(0) + along_0(1)


def shards(sizes, hidden, cotangent, blocks, block_pos, owner_rank, moment, second):
    tokens, feats = cotangent.shape
    rows = hidden.shape[1]
    slots, bs, _ = blocks.shape
    n0, n1, nx, nc = sizes
    width = feats * nx * nc
    axes = (*DP, *TENSOR)
    first, then = chip_groups(sizes)
    place = jnp.stack([lax.axis_index("x"), lax.axis_index("core"), lax.axis_index(DP)])
    swap = [(0, 1), (1, 0)]
    factor = 1.0 / (tokens * n0 * n1)
    block_list = jax.ShapeDtypeStruct((slots, bs, bs), BF)

    def exchange(value, groups):
        return lax.all_to_all(value, axes, 0, 0, axis_index_groups=groups, tiled=True)

    own = lax.all_to_all(jnp.broadcast_to(cotangent, (nx, tokens, feats)), "x", 0, 0, tiled=True)
    keep, send, mine, hid_t = call(
        partial_kernel,
        (*(jax.ShapeDtypeStruct((nx, tokens, feats), BF),) * 2, jax.ShapeDtypeStruct((bs, bs), BF), jax.ShapeDtypeStruct((rows, tokens), BF)),
        [SMEM, SMEM, SMEM, VMEM, VMEM],
        [VMEM] * 4,
        [pltpu.VMEM((rows, width), BF)],
        flops=2 * tokens * rows * width,
        nbytes=4 * 2**20,
        limit=60,
    )(place, block_pos, owner_rank, hidden, blocks)
    swapped = lax.ppermute(send, "core", swap)
    own, keep, swapped = lax.optimization_barrier((own, keep, swapped))
    other = lax.ppermute(own, "core", swap)
    grads = call(
        functools.partial(grads_kernel, n0, factor),
        block_list,
        [SMEM, SMEM, SMEM, VMEM, ANY, ANY],
        ANY,
        [
            pltpu.VMEM((tokens, width), BF),
            pltpu.VMEM((slots, bs, bs), BF),
            pltpu.SemaphoreType.DMA((2, nx)),
            pltpu.SemaphoreType.DMA((slots,)),
        ],
        flops=2 * tokens * bs * bs * slots,
        nbytes=4 * 2**20,
        limit=12,
    )(place, block_pos, owner_rank, hid_t, own, other)
    grads, keep, swapped = lax.optimization_barrier((grads, keep, swapped))
    hidden_grad = call(
        back_kernel,
        jax.ShapeDtypeStruct((tokens, rows), BF),
        [SMEM, SMEM, VMEM, ANY, ANY],
        VMEM,
        [pltpu.VMEM((tokens, width), BF), pltpu.VMEM((rows, width), BF), pltpu.SemaphoreType.DMA((2, nx))],
        flops=2 * tokens * rows * width,
        nbytes=4 * 2**20,
        limit=16,
    )(place, block_pos, blocks, own, other)

    def halved(value, step, beside=None):
        half = value.shape[0] // 2
        theirs = lax.ppermute(value[half:], "x", [(i, i ^ step) for i in range(nx)])
        theirs, beside = lax.optimization_barrier((theirs, beside))
        return (value[:half].astype(F32) + theirs.astype(F32)).astype(BF), beside

    got = exchange(grads.reshape(n0, slots // n0, bs, bs), first)
    total = (keep.astype(F32) + swapped.astype(F32)).astype(BF)
    total, hidden_grad = halved(total, 1, hidden_grad)
    part = got.astype(F32).sum(axis=0).astype(BF)
    part, total = lax.optimization_barrier((part, total))
    step = 2
    while total.shape[0] > 1:
        total, _ = halved(total, step)
        step *= 2
    mixed = total[0]
    grad = exchange(part, then).astype(F32).sum(axis=0)
    weight = mine.astype(F32)
    mom_next = 0.9 * moment[0, 0] + 0.1 * grad
    sec_next = 0.999 * second[0, 0] + 0.001 * grad * grad
    step_dir = mom_next / (jnp.sqrt(sec_next) + 1e-08)
    updated = (weight - 0.002 * (step_dir + 0.1 * weight)).astype(BF)
    row = exchange(jnp.broadcast_to(updated, (n1, bs, bs)), then)
    every = exchange(jnp.broadcast_to(row, (n0, n1, bs, bs)), first)
    new_blocks = call(
        functools.partial(list_kernel, n0),
        block_list,
        [SMEM, SMEM, ANY],
        ANY,
        [pltpu.SemaphoreType.DMA((slots,))],
        nbytes=4 * 2**20,
        limit=4,
    )(place, owner_rank, every.reshape(slots, bs, bs))
    return (mixed, hidden_grad, mom_next[None, None], sec_next[None, None], step_dir[None, None], new_blocks)


def make(sizes, torus):
    placed = (
        P(DP, TENSOR),
        P(DP, TENSOR),
        P(TENSOR, None, None),
        P(TENSOR, None),
        P(TENSOR, None),
        P(TENSOR, DP, None, None),
        P(TENSOR, DP, None, None),
    )
    return jax.shard_map(
        functools.partial(shards, sizes),
        mesh=torus,
        in_specs=placed,
        out_specs=(
            P(DP, TENSOR),
            P(DP, TENSOR),
            P(TENSOR, DP, None, None),
            P(TENSOR, DP, None, None),
            P(TENSOR, DP, None, None),
            P(TENSOR, None, None),
        ),
        check_vma=False,
    )


def solution(mesh):
    sizes = (8, mesh.shape["dp"] // 8, mesh.shape["tensor"] // 2, 2)
    return make(sizes, Mesh(mesh.devices.reshape(sizes), (*DP, *TENSOR)))
```
